32 devices in a mesh: prompt: 1, seq: 32 (over z, y, x, core).
Axes of the slice: x: 2, y: 2, z: 4, core: 2. Of those that a mesh axis runs over, the one named last changes fastest.
Arguments:
- queries: bfloat16 [8192, 32, 128], P(('prompt', 'seq')), may hold values from -12 to 12
- key_value: bfloat16 [2, 8192, 16, 128], P(None, ('prompt', 'seq')), may hold values from -6 to 6
- damping: bfloat16 [8192], P('prompt'), may hold values from 0.0099487305 to 1
- span_start: int32 [1], P('prompt'), may hold values from 0 to 3584
- steered_heads: int32 [8], replicated, may hold values from 0 to 31, as said below
Outputs:
- attention: bfloat16 [8192, 32, 128], P(('prompt', 'seq'))
The draws below stay inside these ranges and needn't reach their ends.
Inputs may be any that keep to these rules, and one draw needn't show every extreme that they name: The emphasized tokens are span_start to span_start + 511. `steered_heads`: 8 distinct head numbers in any order; head 31 is always one of them.
All inputs are finite; a program needn't handle non-finite values.
Results may differ from the reference program's by a relative error of at most 0.0085.
Values may be sent and summed in bfloat16 or wider, within the bound.
A program may use at most 64 MiB of HBM per device.

```python
import math
import jax
import jax.numpy as jnp
from jax import lax

HEADS = 32
KV_HEADS = 16
HEAD_DIM = 128
WINDOW = 4096
SPAN = 512
STEERED = 8
TOKENS = 8192


def draw_steered_heads(key, part):
    others = jax.random.permutation(jax.random.fold_in(key, 11), HEADS - 1)[:STEERED - 1].astype(jnp.int32)
    chosen = jnp.concatenate([others, jnp.full((1,), HEADS - 1, jnp.int32)])
    order = jax.random.permutation(jax.random.fold_in(key, 23), STEERED)
    return chosen[order].astype(jnp.int32)


def shard_levels(own_key, shape, shards, least, high):
    loudness = 1.0
    for axis_at, blocks in shards:
        heights = jax.random.uniform(jax.random.fold_in(jax.random.fold_in(own_key, 6), axis_at), (blocks,), jnp.float32, least / len(shards), high / len(shards))
        loudness = loudness * jnp.repeat(jnp.exp(heights), shape[axis_at] // blocks).reshape((-1,) + (1,) * (len(shape) - 1 - axis_at))
    return loudness


def centred(rng, dims, spread, bound, split=(), held_as=jnp.bfloat16):
    factor_of = shard_levels(rng, dims, split, -0.22, 0.18) if split else 1.0
    values = jax.random.normal(rng, dims, jnp.float32) * spread * factor_of
    return jnp.minimum(jnp.maximum(values, -bound), bound).astype(held_as)


def setup_inputs(seed: int = 0, part: int = 0) -> dict:
    seeds = jax.random.split(jax.random.key(seed), 6)
    part_keys = jax.random.split(jax.random.fold_in(seeds[5], part), 6)
    queries = centred(part_keys[0], (TOKENS, HEADS, HEAD_DIM), 3.0, 12.0, ((0, 32),))
    key_value = centred(part_keys[1], (2, TOKENS, KV_HEADS, HEAD_DIM), 1.0, 6.0, ((1, 32),))
    damping = jnp.clip(jnp.exp(jax.random.uniform(part_keys[2], (TOKENS,), jnp.float32, math.log(0.0099487305), math.log(1.0))), 0.0099487305, 1.0).astype(jnp.bfloat16)
    span_start = jax.random.randint(part_keys[3], (1,), 0, max(TOKENS - WINDOW - SPAN, 0) + 1).astype(jnp.int32)
    steered_heads = draw_steered_heads(jax.random.fold_in(seeds[5], 71), part)
    return dict(queries=queries, key_value=key_value, damping=damping, span_start=span_start, steered_heads=steered_heads)


SCORE_SCALE = 144.0 ** -0.5
SOFTCAP = 50.0


def piece_terms(query_groups, key_piece, value_piece, key_bias, visible):
    raw_score = jnp.einsum("qkgd,skd->kgqs", query_groups.astype(jnp.float32), key_piece.astype(jnp.float32))
    scores = SOFTCAP * jnp.tanh(raw_score * SCORE_SCALE / SOFTCAP) + key_bias
    weight = jnp.where(visible, jnp.exp(scores), jnp.float32(0.0))
    weight_sum = jnp.sum(weight, axis=-1)
    rounded = weight.astype(jnp.bfloat16)
    weighted = jnp.einsum("kgqs,skd->kgqd", rounded.astype(jnp.float32), value_piece.astype(jnp.float32))
    return weighted, weight_sum


def reference(queries, key_value, damping, span_start, steered_heads):
    total_rows, head_count, head_width = queries.shape
    key_heads = key_value.shape[2]
    group_size = head_count // key_heads
    block_rows = min(512, total_rows)
    span_first = span_start[0].astype(jnp.int32)
    head_index = jnp.arange(head_count, dtype=jnp.int32)
    steered = jnp.any(steered_heads[:, None] == head_index[None, :], axis=0)
    steer_grid = steered.reshape(key_heads, group_size)[:, :, None, None]
    log_damping = jnp.log(damping.astype(jnp.float32))
    padded_states = jnp.pad(key_value, ((0, 0), (WINDOW, 0), (0, 0), (0, 0)))
    padded_log = jnp.pad(log_damping, (WINDOW, 0))
    span_states = lax.dynamic_slice_in_dim(key_value, span_first, SPAN, 1)
    span_index = span_first + jnp.arange(SPAN, dtype=jnp.int32)

    def one_block(block_index):
        first_row = (block_index * block_rows).astype(jnp.int32)
        query_index = first_row + jnp.arange(block_rows, dtype=jnp.int32)
        query_groups = lax.dynamic_slice_in_dim(queries, first_row, block_rows, 0).reshape(block_rows, key_heads, group_size, head_width)
        window_states = lax.dynamic_slice_in_dim(padded_states, first_row, WINDOW + block_rows, 1)
        window_log = lax.dynamic_slice_in_dim(padded_log, first_row, WINDOW + block_rows, 0)
        key_index = first_row - WINDOW + jnp.arange(WINDOW + block_rows, dtype=jnp.int32)
        emphasis = (key_index >= span_first) & (key_index < span_first + SPAN)
        distance = query_index[:, None] - key_index[None, :]
        visible = (key_index[None, :] >= 0) & (distance >= 0) & (distance < WINDOW)
        key_bias = jnp.where(steer_grid & ~emphasis[None, None, None, :], window_log[None, None, None, :], jnp.float32(0.0))
        weighted, weight_sum = piece_terms(query_groups, window_states[0], window_states[1], key_bias, visible[None, None])
        span_distance = query_index[:, None] - span_index[None, :]
        span_visible = steer_grid & (span_distance >= WINDOW)[None, None]
        more_weighted, more_sum = piece_terms(query_groups, span_states[0], span_states[1], jnp.float32(0.0), span_visible)
        result = (weighted + more_weighted) / (weight_sum + more_sum)[..., None]
        result = result.astype(jnp.bfloat16)
        return result.transpose(2, 0, 1, 3).reshape(block_rows, head_count, head_width)

    outputs = lax.map(one_block, jnp.arange(total_rows // block_rows, dtype=jnp.int32))
    return outputs.reshape(total_rows, head_count, head_width)
```

```python
import functools

import jax
import jax.numpy as jnp
from jax import lax
from jax.experimental import pallas as pl
from jax.experimental.pallas import tpu as pltpu
from jax.sharding import PartitionSpec as P

WINDOW = 4096
SPAN = 512
SCORE_SCALE = 144.0 ** (-0.5)
SOFTCAP = 50.0
LOG2E = 1.4426950408889634
BLOCK = 512
REACH = 2
HIDDEN = -1e30
MESH = pl.DeviceIdType.MESH


def dot_t(q, k):
    return lax.dot_general(q, k, (((1,), (1,)), ((), ())), preferred_element_type=jnp.float32)


def attend(
    plane_size, planes,
    span_ref, steer_ref, damp_ref, q_in, kv_in, out_ref,
    q_ref, kv_ref, span_src, span_dst, acc, done, bias, span_bias,
    q_send, q_recv, own_send, own_recv, up_send, up_recv, span_send, span_recv, out_send, out_recv,
):
    me = lax.axis_index("seq")
    plane = me // plane_size
    place = lax.rem(me, plane_size)
    chunk = q_in.shape[1]
    rows = plane_size * chunk
    blocks = rows // BLOCK
    per_block = BLOCK // chunk
    heads = q_ref.shape[0]
    groups = kv_ref.shape[0]
    share = heads // groups
    width = q_ref.shape[2]
    has_below = plane > 0
    has_above = plane < planes - 1

    def mate(other):
        return {"seq": plane * plane_size + other}

    def q_copy(group, target, sender):
        return pltpu.make_async_remote_copy(
            src_ref=q_in.at[pl.ds(target * heads + group * share, share)],
            dst_ref=q_ref.at[pl.ds(group * share, share), pl.ds(sender * chunk, chunk)],
            send_sem=q_send.at[group, target],
            recv_sem=q_recv.at[group, sender],
            device_id=mate(target),
            device_id_type=MESH,
        )

    def q_own(group):
        return pltpu.make_async_copy(
            q_in.at[pl.ds(place * heads + group * share, share)],
            q_ref.at[pl.ds(group * share, share), pl.ds(place * chunk, chunk)],
            q_recv.at[group, place],
        )

    def chunk_rows(slot, at):
        return pl.ds(slot * rows + at * chunk, chunk)

    def own_copy(group, target, sender):
        return pltpu.make_async_remote_copy(
            src_ref=kv_in.at[target * groups + group],
            dst_ref=kv_ref.at[group, :, chunk_rows(REACH, sender)],
            send_sem=own_send.at[group, target],
            recv_sem=own_recv.at[group, sender],
            device_id=mate(target),
            device_id_type=MESH,
        )

    def own_local(group):
        return pltpu.make_async_copy(
            kv_in.at[place * groups + group],
            kv_ref.at[group, :, chunk_rows(REACH, place)],
            own_recv.at[group, place],
        )

    def up_copy(slot, group, at, source=None):
        return pltpu.make_async_remote_copy(
            src_ref=kv_ref.at[group, :, chunk_rows(slot, at)] if source is None else source,
            dst_ref=kv_ref.at[group, :, chunk_rows(slot - 1, at)],
            send_sem=up_send.at[slot - 1, group, at],
            recv_sem=up_recv.at[slot - 1, group, at],
            device_id={"seq": me + plane_size},
            device_id_type=MESH,
        )

    def up_first(group):
        return up_copy(REACH, group, place, kv_in.at[place * groups + group])

    def span_copy(group):
        return pltpu.make_async_remote_copy(
            src_ref=span_src.at[group],
            dst_ref=span_dst.at[group],
            send_sem=span_send.at[group],
            recv_sem=span_recv.at[group],
            device_id={"seq": me + plane_size},
            device_id_type=MESH,
        )

    def out_copy(group, target, sender):
        return pltpu.make_async_remote_copy(
            src_ref=done.at[pl.ds(group * share, share), pl.ds(target * chunk, chunk)],
            dst_ref=out_ref.at[pl.ds(sender * heads + group * share, share)],
            send_sem=out_send.at[group, target],
            recv_sem=out_recv.at[group, sender],
            device_id=mate(target),
            device_id_type=MESH,
        )

    def out_own(group):
        return pltpu.make_async_copy(
            done.at[pl.ds(group * share, share), pl.ds(place * chunk, chunk)],
            out_ref.at[pl.ds(place * heads + group * share, share)],
            out_recv.at[group, place],
        )

    barrier = pltpu.get_barrier_semaphore()

    @pl.loop(1, plane_size)
    def _(step):
        other = lax.rem(place + step, plane_size)
        pl.semaphore_signal(barrier, inc=1, device_id=mate(other), device_id_type=MESH)

    @pl.when(has_below)
    def _():
        pl.semaphore_signal(
            barrier, inc=1, device_id={"seq": me - plane_size}, device_id_type=MESH
        )

    @pl.when(has_above)
    def _():
        pl.semaphore_signal(
            barrier, inc=1, device_id={"seq": me + plane_size}, device_id_type=MESH
        )

    below, above = (plane + planes - 1) // planes, (2 * planes - 2 - plane) // planes
    pl.semaphore_wait(barrier, plane_size - 1 + below + above)

    for group in range(groups):

        @pl.when(has_above)
        def _():
            up_first(group).start()

        own_local(group).start()

        @pl.loop(1, plane_size)
        def _(step):
            own_copy(group, lax.rem(place + step, plane_size), place).start()

        q_own(group).start()

        @pl.loop(1, plane_size)
        def _(step):
            q_copy(group, lax.rem(place + step, plane_size), place).start()

    log_damping = jnp.log(damp_ref[...].astype(jnp.float32)) * LOG2E
    index = lax.broadcasted_iota(jnp.int32, log_damping.shape, 0) * BLOCK
    index += lax.broadcasted_iota(jnp.int32, log_damping.shape, 1)
    first = span_ref[...]
    emphasis = (index >= first) & (index < first + SPAN)
    kept_first = jnp.minimum(first, rows - SPAN)
    kept = kept_first + lax.broadcasted_iota(jnp.int32, (1, SPAN), 1)
    kept_emphasis = (kept >= first) & (kept < first + SPAN)
    for head in range(heads):
        steered = jnp.max(
            jnp.where(steer_ref[...] == place * heads + head, 1.0, 0.0), axis=1, keepdims=True
        )
        inside = jnp.where(emphasis, 0.0, log_damping * steered)
        beyond = jnp.where(emphasis, (1.0 - steered) * HIDDEN, HIDDEN)
        for block in range(log_damping.shape[0]):
            bias[0, head, block] = inside[block : block + 1]
            bias[1, head, block] = beyond[block : block + 1]
        span_bias[head] = jnp.where(kept_emphasis, (1.0 - steered) * HIDDEN, HIDDEN)

    acc[...] = jnp.zeros_like(acc)
    ones = jnp.ones((BLOCK, width), jnp.bfloat16)
    gap = lax.broadcasted_iota(jnp.int32, (BLOCK, BLOCK), 1) - lax.broadcasted_iota(
        jnp.int32, (BLOCK, BLOCK), 0
    )

    def add(group, row_block, k, v, bias_of):
        both = jnp.concatenate([v, ones], axis=1)
        here = pl.ds(pl.multiple_of(row_block * BLOCK, BLOCK), BLOCK)
        for member in range(share):
            head = group * share + member
            raw = dot_t(q_ref[head, here, :], k)
            capped = jnp.tanh(raw * (SCORE_SCALE / SOFTCAP)) * (SOFTCAP * LOG2E)
            weight = jnp.exp2(capped + bias_of(head)).astype(jnp.bfloat16)
            acc[head, here, :] += jnp.dot(weight, both, preferred_element_type=jnp.float32)

    def add_block(group, row_block, slot, key_block, bias_of):
        there = pl.ds(pl.multiple_of(slot * rows + key_block * BLOCK, BLOCK), BLOCK)
        add(group, row_block, kv_ref[group, 0, there, :], kv_ref[group, 1, there, :], bias_of)

    def wait_own(group, at):
        @pl.when(at == place)
        def _():
            own_local(group).wait()

        @pl.when(at != place)
        def _():
            own_copy(group, at, at).wait_recv()

            @pl.when(has_above)
            def _():
                up_copy(REACH, group, at).start()

    @pl.loop(0, groups)
    def _(group):
        def wait_q(at):
            @pl.when(at == place)
            def _():
                q_own(group).wait()

            @pl.when(at != place)
            def _():
                q_copy(group, at, at).wait_recv()

        def global_block(slot, key_block):
            return (plane - REACH + slot) * blocks + key_block

        @pl.loop(0, blocks)
        def _(key_block):
            for part in range(per_block):
                wait_own(group, key_block * per_block + part)

            @pl.when(key_block == 0)
            def _():
                pl.loop(0, plane_size)(wait_q)

            at = global_block(REACH, key_block)
            add_block(
                group, key_block, REACH, key_block,
                lambda head: jnp.where(gap <= 0, bias[0, head, at], HIDDEN),
            )

            @pl.loop(key_block + 1, blocks)
            def _(row_block):
                add_block(group, row_block, REACH, key_block, lambda head: bias[0, head, at])

        @pl.when(plane >= 1)
        def _():
            @pl.loop(0, blocks)
            def _(key_block):
                for part in range(per_block):
                    where = key_block * per_block + part
                    up_copy(REACH, group, where).wait_recv()

                    @pl.when(has_above)
                    def _():
                        up_copy(REACH - 1, group, where).start()

                at = global_block(REACH - 1, key_block)

                @pl.loop(0, blocks)
                def _(row_block):
                    add_block(
                        group, row_block, REACH - 1, key_block, lambda head: bias[0, head, at]
                    )

        @pl.when(plane >= 2)
        def _():
            @pl.loop(0, blocks)
            def _(key_block):
                for part in range(per_block):
                    up_copy(REACH - 1, group, key_block * per_block + part).wait_recv()
                at = global_block(0, key_block)
                add_block(
                    group, key_block, 0, key_block,
                    lambda head: jnp.where(gap > 0, bias[0, head, at], bias[1, head, at]),
                )

                @pl.loop(1, blocks)
                def _(step):
                    row_block = lax.rem(key_block + step, blocks)
                    beyond = (row_block + blocks - key_block - step) // blocks
                    add_block(
                        group, row_block, 0, key_block,
                        lambda head: bias[beyond, head, at],
                    )

        @pl.when(plane == 2)
        def _():
            for half in range(2):
                picked = jnp.zeros((SPAN, width), jnp.float32)
                for part in range(blocks):
                    wanted = kept_first + lax.broadcasted_iota(jnp.int32, (SPAN, BLOCK), 0)
                    key = lax.broadcasted_iota(jnp.int32, (SPAN, BLOCK), 1) + part * BLOCK
                    pick = jnp.where(wanted == key, 1.0, 0.0).astype(jnp.bfloat16)
                    picked += jnp.dot(
                        pick,
                        kv_ref[group, half, part * BLOCK : (part + 1) * BLOCK, :],
                        preferred_element_type=jnp.float32,
                    )
                span_src[group, half] = picked.astype(jnp.bfloat16)
            span_copy(group).start()

        @pl.when(plane == 3)
        def _():
            span_copy(group).wait_recv()

            @pl.loop(0, blocks)
            def _(row_block):
                add(
                    group, row_block, span_dst[group, 0], span_dst[group, 1],
                    lambda head: span_bias[head],
                )

        @pl.loop(0, blocks)
        def _(row_block):
            here = pl.ds(pl.multiple_of(row_block * BLOCK, BLOCK), BLOCK)
            for member in range(share):
                head = group * share + member
                total = acc[head, here, :]
                done[head, here, :] = (total[:, :width] / total[:, width:]).astype(done.dtype)
            for part in range(per_block):
                target = row_block * per_block + part

                @pl.when(target == place)
                def _():
                    out_own(group).start()

                @pl.when(target != place)
                def _():
                    out_copy(group, target, place).start()

    @pl.loop(0, groups)
    def _(group):
        out_own(group).wait()

        @pl.loop(1, plane_size)
        def _(step):
            other = lax.rem(place + step, plane_size)
            own_copy(group, other, place).wait_send()
            q_copy(group, other, place).wait_send()
            out_copy(group, other, place).wait_send()
            out_copy(group, other, other).wait_recv()

        @pl.when(has_above)
        def _():
            @pl.loop(0, plane_size)
            def _(at):
                up_copy(REACH, group, at).wait_send()

        @pl.when(has_above & has_below)
        def _():
            @pl.loop(0, plane_size)
            def _(at):
                up_copy(REACH - 1, group, at).wait_send()

        @pl.when(plane == 2)
        def _():
            span_copy(group).wait_send()


def per_device(queries, key_value, damping, span_start, steered_heads):
    chunk, head_count, width = queries.shape
    key_heads = key_value.shape[2]
    total_rows = damping.shape[0]
    devices = lax.axis_size("seq")
    plane_size = WINDOW // REACH // chunk
    planes = devices // plane_size
    rows = plane_size * chunk
    heads = head_count // plane_size
    groups = key_heads // plane_size
    pairs = heads * rows * WINDOW
    moved = pl.pallas_call(
        functools.partial(attend, plane_size, planes),
        out_shape=jax.ShapeDtypeStruct((head_count, chunk, width), jnp.bfloat16),
        in_specs=[pl.BlockSpec(memory_space=pltpu.VMEM)] * 5,
        out_specs=pl.BlockSpec(memory_space=pl.ANY),
        scratch_shapes=[
            pltpu.VMEM((heads, rows, width), jnp.bfloat16),
            pltpu.VMEM((groups, 2, (REACH + 1) * rows, width), jnp.bfloat16),
            pltpu.VMEM((groups, 2, SPAN, width), jnp.bfloat16),
            pltpu.VMEM((groups, 2, SPAN, width), jnp.bfloat16),
            pltpu.VMEM((heads, rows, 2 * width), jnp.float32),
            pltpu.VMEM((heads, rows, width), jnp.bfloat16),
            pltpu.VMEM((2, heads, total_rows // BLOCK, 1, BLOCK), jnp.float32),
            pltpu.VMEM((heads, 1, SPAN), jnp.float32),
            pltpu.SemaphoreType.DMA((groups, plane_size)),
            pltpu.SemaphoreType.DMA((groups, plane_size)),
            pltpu.SemaphoreType.DMA((groups, plane_size)),
            pltpu.SemaphoreType.DMA((groups, plane_size)),
            pltpu.SemaphoreType.DMA((REACH, groups, plane_size)),
            pltpu.SemaphoreType.DMA((REACH, groups, plane_size)),
            pltpu.SemaphoreType.DMA((groups,)),
            pltpu.SemaphoreType.DMA((groups,)),
            pltpu.SemaphoreType.DMA((groups, plane_size)),
            pltpu.SemaphoreType.DMA((groups, plane_size)),
        ],
        compiler_params=pltpu.CompilerParams(
            collective_id=0, has_side_effects=True, vmem_limit_bytes=56 * 1024 * 1024
        ),
        cost_estimate=pl.CostEstimate(
            flops=6 * pairs * width, transcendentals=2 * pairs, bytes_accessed=6 * chunk * head_count * width
        ),
        name="attend",
    )(
        span_start.reshape(1, 1),
        steered_heads.reshape(1, -1),
        damping.reshape(-1, BLOCK),
        queries.transpose(1, 0, 2),
        key_value.transpose(2, 0, 1, 3),
    )
    return moved.transpose(1, 0, 2)


def solution(mesh):
    in_specs = (
        P(("prompt", "seq"), None, None),
        P(None, ("prompt", "seq"), None, None),
        P("prompt"),
        P("prompt"),
        P(),
    )
    out_specs = P(("prompt", "seq"), None, None)
    return jax.shard_map(
        per_device, mesh=mesh, in_specs=in_specs, out_specs=out_specs, check_vma=False
    )
```

```python
import functools

import jax
import jax.numpy as jnp
from jax import lax
from jax.experimental import pallas as pl
from jax.experimental.pallas import tpu as pltpu
from jax.sharding import PartitionSpec as P

WINDOW = 4096
SPAN = 512
SCORE_SCALE = 144.0 ** (-0.5)
SOFTCAP = 50.0
LOG2E = 1.4426950408889634
BLOCK = 512
REACH = 2
CORES = 2
WAITING = 4
HIDDEN = -1e30
MESH = pl.DeviceIdType.MESH


def dot_t(q, k):
    return lax.dot_general(q, k, (((1,), (1,)), ((), ())), preferred_element_type=jnp.float32)


def attend(
    plane_size, planes,
    span_ref, steer_ref, damp_ref, q_in, kv_in, out_ref,
    q_ref, kv_ref, span_src, span_dst, acc, done, bias, span_bias, pick,
    q_send, q_recv, own_send, mate_send, up_send, kv_recv,
    span_send, span_mate, span_recv, out_send, out_recv,
):
    me = lax.axis_index("seq")
    plane = me // plane_size
    place = lax.rem(me, plane_size)
    chip, core = place // CORES, lax.rem(place, CORES)
    chips = plane_size // CORES
    chunk = q_in.shape[1]
    rows = plane_size * chunk
    blocks = rows // BLOCK
    per_block = BLOCK // chunk
    held = blocks // CORES
    heads, _, width = q_ref.shape
    groups = kv_ref.shape[0]
    share = heads // groups
    has_below = plane > 0
    has_above = plane < planes - 1

    def block_of(turn):
        return core + turn * (blocks - 1 - 2 * core)

    def owner(row_block):
        return lax.rem((row_block + 1) // 2, CORES)

    def held_rows(at):
        return pl.ds(at // per_block // CORES * BLOCK + lax.rem(at, per_block) * chunk, chunk)

    def at_place(other):
        return {"seq": plane * plane_size + other}

    mate = at_place(chip * CORES + 1 - core)
    above = {"seq": me + plane_size}

    def remote(source, target, send_sem, recv_sem, device):
        return pltpu.make_async_remote_copy(
            src_ref=source,
            dst_ref=target,
            send_sem=send_sem,
            recv_sem=recv_sem,
            device_id=device,
            device_id_type=MESH,
        )

    def of_group(group):
        return pl.ds(group * share, share)

    def q_source(group, other):
        return q_in.at[pl.ds(other * heads + group * share, share)]

    def q_copy(group, other, at):
        return remote(
            q_source(group, other),
            q_ref.at[of_group(group), held_rows(at)],
            q_send.at[group, other],
            q_recv.at[group, at],
            at_place(other * CORES + owner(at // per_block)),
        )

    def q_own(group):
        return pltpu.make_async_copy(
            q_source(group, chip),
            q_ref.at[of_group(group), held_rows(place)],
            q_recv.at[group, place],
        )

    def keys_at(slot, group, at):
        return kv_ref.at[group, :, pl.ds(slot * rows + at * chunk, chunk)]

    def own_copy(group, other, at):
        return remote(
            kv_in.at[other * groups + group],
            keys_at(REACH, group, at),
            own_send.at[group, other],
            kv_recv.at[REACH, group, at],
            at_place(other * CORES + core),
        )

    def own_local(group):
        return pltpu.make_async_copy(
            kv_in.at[chip * groups + group],
            keys_at(REACH, group, place),
            kv_recv.at[REACH, group, place],
        )

    def mate_copy(slot, group, at, source=None):
        return remote(
            keys_at(slot, group, at) if source is None else source,
            keys_at(slot, group, at),
            mate_send.at[slot, group, at],
            kv_recv.at[slot, group, at],
            mate,
        )

    def up_copy(slot, group, at, source=None):
        return remote(
            keys_at(slot, group, at) if source is None else source,
            keys_at(slot - 1, group, at),
            up_send.at[slot - 1, group, at],
            kv_recv.at[slot - 1, group, at],
            above,
        )

    def span_up(group):
        return remote(
            span_src.at[group],
            span_dst.at[group, core],
            span_send.at[group],
            span_recv.at[group, core],
            above,
        )

    def span_over(group, half):
        return remote(
            span_dst.at[group, half],
            span_dst.at[group, half],
            span_mate.at[group],
            span_recv.at[group, half],
            mate,
        )

    def out_copy(group, at, sender):
        return remote(
            done.at[of_group(group), held_rows(at)],
            out_ref.at[pl.ds(sender * heads + group * share, share)],
            out_send.at[group, at],
            out_recv.at[group, sender],
            at_place(at),
        )

    def out_own(group):
        return pltpu.make_async_copy(
            done.at[of_group(group), held_rows(place)],
            out_ref.at[pl.ds(chip * heads + group * share, share)],
            out_recv.at[group, chip],
        )

    barrier = pltpu.get_barrier_semaphore()

    def greet(device):
        pl.semaphore_signal(barrier, inc=1, device_id=device, device_id_type=MESH)

    @pl.loop(1, plane_size)
    def _(step):
        greet(at_place(lax.rem(place + step, plane_size)))

    @pl.when(has_below)
    def _():
        greet({"seq": me - plane_size})

    @pl.when(has_above)
    def _():
        greet(above)

    neighbours = (plane + planes - 1) // planes + (2 * planes - 2 - plane) // planes
    pl.semaphore_wait(barrier, plane_size - 1 + neighbours)

    q_owner = owner(place // per_block)

    def exchange_keys(group):
        @pl.loop(1, chips)
        def _(step):
            own_copy(group, lax.rem(chip + step, chips), place).start()

        own_local(group).start()
        mate_copy(REACH, group, place, kv_in.at[chip * groups + group]).start()

    def exchange_queries(group):
        @pl.loop(1, chips)
        def _(step):
            q_copy(group, lax.rem(chip + step, chips), place).start()

        @pl.when(q_owner == core)
        def _():
            q_own(group).start()

        @pl.when(q_owner != core)
        def _():
            q_copy(group, chip, place).start()

    def send_up(slot, group, turn):
        @pl.when(turn >= WAITING)
        def _():
            up_copy(slot, group, (turn - WAITING) * CORES + core).wait_send()

        @pl.when((turn < WAITING) & (group > 0))
        def _():
            earlier = turn + chips - WAITING
            up_copy(slot, group - 1, earlier * CORES + core).wait_send()

        up_copy(slot, group, turn * CORES + core).start()

    def pass_own(group, turn):
        mine = turn * CORES + core

        @pl.when(mine == place)
        def _():
            own_local(group).wait()

        @pl.when(mine != place)
        def _():
            own_copy(group, chip, mine).wait_recv()
            mate_copy(REACH, group, mine).start()

        @pl.when(has_above)
        def _():
            send_up(REACH, group, turn)

    def pass_later(slot, group, turn):
        mine = turn * CORES + core
        up_copy(slot + 1, group, mine).wait_recv()
        mate_copy(slot, group, mine).start()
        if slot > 0:

            @pl.when(has_above)
            def _():
                send_up(slot, group, turn)

    def await_mate(slot, group, turn):
        mate_copy(slot, group, turn * CORES + 1 - core).wait_recv()

    exchange_keys(0)

    @pl.loop(0, blocks)
    def _(turn):
        pass_own(0, turn)

    exchange_queries(0)
    exchange_keys(1)
    exchange_queries(1)

    log_damping = jnp.log(damp_ref[...].astype(jnp.float32)) * LOG2E
    index = lax.broadcasted_iota(jnp.int32, log_damping.shape, 0) * width
    index += lax.broadcasted_iota(jnp.int32, log_damping.shape, 1)
    first = span_ref[...]
    emphasis = (index >= first) & (index < first + SPAN)
    kept_first = jnp.minimum(first, rows - SPAN)
    kept = kept_first + lax.broadcasted_iota(jnp.int32, (1, SPAN), 1)
    kept_emphasis = (kept >= first) & (kept < first + SPAN)
    for head in range(heads):
        steered = jnp.max(
            jnp.where(steer_ref[...] == chip * heads + head, 1.0, 0.0), axis=1, keepdims=True
        )
        inside = jnp.where(emphasis, 0.0, log_damping * steered)
        beyond = jnp.where(emphasis, (1.0 - steered) * HIDDEN, HIDDEN)
        bias[0, head] = inside
        bias[1, head] = beyond
        span_bias[head] = jnp.where(kept_emphasis, (1.0 - steered) * HIDDEN, HIDDEN)

    @pl.when(plane == REACH)
    def _():
        for part in range(blocks):
            wanted = kept_first + lax.broadcasted_iota(jnp.int32, (SPAN, BLOCK), 0)
            key = lax.broadcasted_iota(jnp.int32, (SPAN, BLOCK), 1) + part * BLOCK
            pick[part] = jnp.where(wanted == key, 1.0, 0.0).astype(pick.dtype)

    acc[...] = jnp.zeros_like(acc)

    ones = jnp.ones((BLOCK, width), jnp.bfloat16)
    gap = lax.broadcasted_iota(jnp.int32, (BLOCK, BLOCK), 1) - lax.broadcasted_iota(
        jnp.int32, (BLOCK, BLOCK), 0
    )

    def add(group, turns, k, v, bias_row):
        both = jnp.concatenate([v, ones], axis=1)
        for turn in turns:
            here = pl.ds(pl.multiple_of(turn * BLOCK, BLOCK), BLOCK)
            for member in range(share):
                head = group * share + member
                raw = dot_t(q_ref[head, here, :], k)
                capped = jnp.tanh(raw * (SCORE_SCALE / SOFTCAP)) * (SOFTCAP * LOG2E)
                weight = jnp.exp2(capped + bias_row(head)).astype(jnp.bfloat16)
                acc[head, here, :] += jnp.dot(weight, both, preferred_element_type=jnp.float32)

    def add_block(group, turns, slot, key_block, bias_row):
        there = pl.ds(pl.multiple_of(slot * rows + key_block * BLOCK, BLOCK), BLOCK)
        add(group, turns, kv_ref[group, 0, there, :], kv_ref[group, 1, there, :], bias_row)

    def finish(group):
        @pl.when(plane == REACH + 1)
        def _():
            span_up(group).wait_recv()
            span_over(group, core).start()
            span_over(group, 1 - core).wait_recv()
            add(
                group, range(held), span_dst[group, 0], span_dst[group, 1],
                lambda head: span_bias[head],
            )

        @pl.loop(0, held)
        def _(turn):
            here = pl.ds(pl.multiple_of(turn * BLOCK, BLOCK), BLOCK)
            for member in range(share):
                head = group * share + member
                total = acc[head, here, :]
                done[head, here, :] = (total[:, :width] / total[:, width:]).astype(done.dtype)
            for part in range(per_block):
                at = block_of(turn) * per_block + part

                @pl.when(at == place)
                def _():
                    out_own(group).start()

                @pl.when(at != place)
                def _():
                    out_copy(group, at, chip).start()

    def global_block(slot, key_block):
        return (plane - REACH + slot) * blocks + key_block

    def bias_of(kind, head, where):
        count = BLOCK // width
        return jnp.concatenate(
            [bias[kind, head, pl.ds(where * count + part, 1), :] for part in range(count)], axis=1
        )

    def await_queries(group):
        @pl.loop(0, held * per_block)
        def _(n):
            at = block_of(n // per_block) * per_block + lax.rem(n, per_block)

            @pl.when(at == place)
            def _():
                q_own(group).wait()

            @pl.when(at != place)
            def _():
                q_copy(group, chip, at).wait_recv()

        @pl.when(group + 2 < groups)
        def _():
            exchange_keys(group + 2)
            exchange_queries(group + 2)

    def same_plane(group, key_block):
        await_mate(REACH, group, key_block)
        where = global_block(REACH, key_block)

        @pl.loop(0, held)
        def _(turn):
            @pl.when(block_of(turn) == key_block)
            def _():
                add_block(
                    group, [turn], REACH, key_block,
                    lambda head: jnp.where(gap <= 0, bias_of(0, head, where), HIDDEN),
                )

            @pl.when(block_of(turn) > key_block)
            def _():
                add_block(group, [turn], REACH, key_block, lambda head: bias_of(0, head, where))

    def next_plane(group, key_block):
        await_mate(REACH - 1, group, key_block)
        where = global_block(REACH - 1, key_block)
        add_block(group, range(held), REACH - 1, key_block, lambda head: bias_of(0, head, where))

    def hand_on(group):
        picked = jnp.zeros((SPAN, width), jnp.float32)
        for part in range(blocks):
            picked += jnp.dot(
                pick[part],
                kv_ref[group, core, part * BLOCK : (part + 1) * BLOCK, :],
                preferred_element_type=jnp.float32,
            )
        span_src[group] = picked.astype(jnp.bfloat16)
        span_up(group).start()

    def far_plane(group, key_block):
        await_mate(0, group, key_block)

        pl.when((plane == REACH) & (key_block == blocks - 1))(functools.partial(hand_on, group))

        where = global_block(0, key_block)

        @pl.loop(0, held)
        def _(turn):
            row_block = block_of(turn)

            @pl.when(row_block == key_block)
            def _():
                add_block(
                    group, [turn], 0, key_block,
                    lambda head: jnp.where(gap > 0, bias_of(0, head, where), bias_of(1, head, where)),
                )

            @pl.when(row_block != key_block)
            def _():
                beyond = (row_block + blocks - key_block) // blocks
                add_block(group, [turn], 0, key_block, lambda head: bias_of(beyond, head, where))

    far = plane // REACH
    late = jnp.maximum(plane - 1, 0)

    @pl.loop(0, groups + REACH)
    def _(round_):
        fresh = round_ < groups

        @pl.when(fresh)
        def _():
            await_queries(round_)

        @pl.loop(0, blocks)
        def _(key_block):
            @pl.when(fresh)
            def _():
                @pl.when(has_below)
                def _():
                    pass_later(REACH - 1, round_, key_block)

            @pl.when((far > 0) & (round_ > 0) & (round_ <= groups))
            def _():
                pass_later(0, round_ - 1, key_block)

            @pl.when(fresh)
            def _():
                same_plane(round_, key_block)

                @pl.when(has_below)
                def _():
                    next_plane(round_, key_block)

            @pl.when(round_ + 1 < groups)
            def _():
                pass_own(round_ + 1, key_block)

            @pl.when((far > 0) & (round_ > 0) & (round_ <= groups))
            def _():
                far_plane(round_ - 1, key_block)

        group = round_ - late
        pl.when((group >= 0) & (group < groups))(functools.partial(finish, group))

    @pl.when(has_above)
    def _():
        @pl.loop(chips - WAITING, chips)
        def _(turn):
            up_copy(REACH, groups - 1, turn * CORES + core).wait_send()

            @pl.when(has_below)
            def _():
                up_copy(REACH - 1, groups - 1, turn * CORES + core).wait_send()

    @pl.loop(0, groups)
    def _(group):
        @pl.loop(1, chips)
        def _(step):
            other = lax.rem(chip + step, chips)
            own_copy(group, other, place).wait_send()
            q_copy(group, other, place).wait_send()
            out_copy(group, place, other).wait_recv()

        @pl.when(q_owner != core)
        def _():
            q_copy(group, chip, place).wait_send()
            out_copy(group, place, chip).wait_recv()

        @pl.when(q_owner == core)
        def _():
            out_own(group).wait()

        @pl.loop(0, held * per_block)
        def _(n):
            at = block_of(n // per_block) * per_block + lax.rem(n, per_block)

            @pl.when(at != place)
            def _():
                out_copy(group, at, chip).wait_send()

        @pl.loop(0, chips)
        def _(n):
            at = n * CORES + core
            mate_copy(REACH, group, at).wait_send()

            @pl.when(has_below)
            def _():
                mate_copy(REACH - 1, group, at).wait_send()

            @pl.when(plane >= REACH)
            def _():
                mate_copy(0, group, at).wait_send()

        @pl.when(plane == REACH)
        def _():
            span_up(group).wait_send()

        @pl.when(plane == REACH + 1)
        def _():
            span_over(group, core).wait_send()


def per_device(queries, key_value, damping, span_start, steered_heads):
    chunk, head_count, width = queries.shape
    key_heads = key_value.shape[2]
    total_rows = damping.shape[0]
    devices = lax.axis_size("seq")
    plane_size = WINDOW // REACH // chunk
    planes = devices // plane_size
    rows = plane_size * chunk
    held_rows = rows // CORES
    chips = plane_size // CORES
    heads = head_count // chips
    groups = key_heads // chips
    pairs = heads * held_rows * WINDOW
    dma = pltpu.SemaphoreType.DMA
    moved = pl.pallas_call(
        functools.partial(attend, plane_size, planes),
        out_shape=jax.ShapeDtypeStruct((head_count, chunk, width), jnp.bfloat16),
        in_specs=[pl.BlockSpec(memory_space=pltpu.VMEM)] * 3 + [pl.BlockSpec(memory_space=pl.ANY)] * 2,
        out_specs=pl.BlockSpec(memory_space=pl.ANY),
        scratch_shapes=[
            pltpu.VMEM((heads, held_rows, width), jnp.bfloat16),
            pltpu.VMEM((groups, 2, (REACH + 1) * rows, width), jnp.bfloat16),
            pltpu.VMEM((groups, SPAN, width), jnp.bfloat16),
            pltpu.VMEM((groups, 2, SPAN, width), jnp.bfloat16),
            pltpu.VMEM((heads, held_rows, 2 * width), jnp.float32),
            pltpu.VMEM((heads, held_rows, width), jnp.bfloat16),
            pltpu.VMEM((2, heads, total_rows // width, width), jnp.float32),
            pltpu.VMEM((heads, 1, SPAN), jnp.float32),
            pltpu.VMEM((rows // BLOCK, SPAN, BLOCK), jnp.bfloat16),
            dma((groups, chips)),
            dma((groups, plane_size)),
            dma((groups, chips)),
            dma((REACH + 1, groups, plane_size)),
            dma((REACH, groups, plane_size)),
            dma((REACH + 1, groups, plane_size)),
            dma((groups,)),
            dma((groups,)),
            dma((groups, 2)),
            dma((groups, plane_size)),
            dma((groups, chips)),
        ],
        compiler_params=pltpu.CompilerParams(
            collective_id=0, has_side_effects=True, vmem_limit_bytes=56 * 1024 * 1024
        ),
        cost_estimate=pl.CostEstimate(
            flops=6 * pairs * width,
            transcendentals=2 * pairs,
            bytes_accessed=6 * chunk * head_count * width,
        ),
        name="attend",
    )(
        span_start.reshape(1, 1),
        steered_heads.reshape(1, -1),
        damping.reshape(-1, width),
        queries.transpose(1, 0, 2),
        key_value.transpose(2, 0, 1, 3),
    )
    return moved.transpose(1, 0, 2)


def solution(mesh):
    in_specs = (
        P(("prompt", "seq"), None, None),
        P(None, ("prompt", "seq"), None, None),
        P("prompt"),
        P("prompt"),
        P(),
    )
    out_specs = P(("prompt", "seq"), None, None)
    return jax.shard_map(
        per_device, mesh=mesh, in_specs=in_specs, out_specs=out_specs, check_vma=False
    )
```

```python
import functools

import jax
import jax.numpy as jnp
from jax import lax
from jax.experimental import pallas as pl
from jax.experimental.pallas import tpu as pltpu
from jax.sharding import PartitionSpec as P

WINDOW = 4096
SPAN = 512
SCORE_SCALE = 144.0 ** (-0.5)
SOFTCAP = 50.0
LOG2E = 1.4426950408889634
BLOCK = 512
REACH = 2
CORES = 2
WAITING = 4
HIDDEN = -1e30
MESH = pl.DeviceIdType.MESH


def dot_t(q, k):
    return lax.dot_general(q, k, (((1,), (1,)), ((), ())), preferred_element_type=jnp.float32)


def attend(
    plane_size, planes,
    span_ref, steer_ref, damp_ref, q_in, kv_in, out_ref,
    q_ref, kv_ref, span_src, span_dst, acc, done, bias, span_bias, pick,
    q_send, q_recv, own_send, mate_send, up_send, kv_recv,
    span_send, span_mate, span_recv, out_send, out_recv,
):
    me = lax.axis_index("seq")
    plane = me // plane_size
    place = lax.rem(me, plane_size)
    chip, core = place // CORES, lax.rem(place, CORES)
    chips = plane_size // CORES
    chunk = q_in.shape[1]
    rows = plane_size * chunk
    blocks = rows // BLOCK
    per_block = BLOCK // chunk
    held = blocks // CORES
    heads, _, width = q_ref.shape
    groups = kv_ref.shape[0]
    share = heads // groups
    has_below = plane > 0
    has_above = plane < planes - 1

    def block_of(turn):
        return core + turn * (blocks - 1 - 2 * core)

    def owner(row_block):
        return lax.rem((row_block + 1) // 2, CORES)

    def held_rows(at):
        return pl.ds(at // per_block // CORES * BLOCK + lax.rem(at, per_block) * chunk, chunk)

    def at_place(other):
        return {"seq": plane * plane_size + other}

    mate = at_place(chip * CORES + 1 - core)
    above = {"seq": me + plane_size}

    def remote(source, target, send_sem, recv_sem, device):
        return pltpu.make_async_remote_copy(
            src_ref=source,
            dst_ref=target,
            send_sem=send_sem,
            recv_sem=recv_sem,
            device_id=device,
            device_id_type=MESH,
        )

    def of_group(group):
        return pl.ds(group * share, share)

    def q_source(group, other):
        return q_in.at[pl.ds(other * heads + group * share, share)]

    def q_copy(group, other, at):
        return remote(
            q_source(group, other),
            q_ref.at[of_group(group), held_rows(at)],
            q_send.at[group, other],
            q_recv.at[group, at],
            at_place(other * CORES + owner(at // per_block)),
        )

    def q_own(group):
        return pltpu.make_async_copy(
            q_source(group, chip),
            q_ref.at[of_group(group), held_rows(place)],
            q_recv.at[group, place],
        )

    def keys_at(slot, group, at):
        return kv_ref.at[group, :, pl.ds(slot * rows + at * chunk, chunk)]

    def own_copy(group, other, at):
        return remote(
            kv_in.at[other * groups + group],
            keys_at(REACH, group, at),
            own_send.at[group, other],
            kv_recv.at[REACH, group, at],
            at_place(other * CORES + core),
        )

    def own_local(group):
        return pltpu.make_async_copy(
            kv_in.at[chip * groups + group],
            keys_at(REACH, group, place),
            kv_recv.at[REACH, group, place],
        )

    def mate_copy(slot, group, at, source=None):
        return remote(
            keys_at(slot, group, at) if source is None else source,
            keys_at(slot, group, at),
            mate_send.at[slot, group, at],
            kv_recv.at[slot, group, at],
            mate,
        )

    def up_copy(slot, group, at, source=None):
        return remote(
            keys_at(slot, group, at) if source is None else source,
            keys_at(slot - 1, group, at),
            up_send.at[slot - 1, group, at],
            kv_recv.at[slot - 1, group, at],
            above,
        )

    def span_up(group):
        return remote(
            span_src.at[group],
            span_dst.at[group, core],
            span_send.at[group],
            span_recv.at[group, core],
            above,
        )

    def span_over(group, half):
        return remote(
            span_dst.at[group, half],
            span_dst.at[group, half],
            span_mate.at[group],
            span_recv.at[group, half],
            mate,
        )

    def out_copy(group, at, sender):
        return remote(
            done.at[of_group(group), held_rows(at)],
            out_ref.at[pl.ds(sender * heads + group * share, share)],
            out_send.at[group, at],
            out_recv.at[group, sender],
            at_place(at),
        )

    def out_own(group):
        return pltpu.make_async_copy(
            done.at[of_group(group), held_rows(place)],
            out_ref.at[pl.ds(chip * heads + group * share, share)],
            out_recv.at[group, chip],
        )

    barrier = pltpu.get_barrier_semaphore()

    def greet(device):
        pl.semaphore_signal(barrier, inc=1, device_id=device, device_id_type=MESH)

    @pl.loop(1, plane_size)
    def _(step):
        greet(at_place(lax.rem(place + step, plane_size)))

    @pl.when(has_below)
    def _():
        greet({"seq": me - plane_size})

    @pl.when(has_above)
    def _():
        greet(above)

    neighbours = (plane + planes - 1) // planes + (2 * planes - 2 - plane) // planes
    pl.semaphore_wait(barrier, plane_size - 1 + neighbours)

    q_owner = owner(place // per_block)

    def exchange_keys(group):
        @pl.loop(1, chips)
        def _(step):
            own_copy(group, lax.rem(chip + step, chips), place).start()

        own_local(group).start()
        mate_copy(REACH, group, place, kv_in.at[chip * groups + group]).start()

    def exchange_queries(group):
        @pl.loop(1, chips)
        def _(step):
            q_copy(group, lax.rem(chip + step, chips), place).start()

        @pl.when(q_owner == core)
        def _():
            q_own(group).start()

        @pl.when(q_owner != core)
        def _():
            q_copy(group, chip, place).start()

    def send_up(slot, group, turn):
        @pl.when(turn >= WAITING)
        def _():
            up_copy(slot, group, (turn - WAITING) * CORES + core).wait_send()

        @pl.when((turn < WAITING) & (group > 0))
        def _():
            earlier = turn + chips - WAITING
            up_copy(slot, group - 1, earlier * CORES + core).wait_send()

        up_copy(slot, group, turn * CORES + core).start()

    def pass_own(group, turn):
        mine = turn * CORES + core

        @pl.when(mine == place)
        def _():
            own_local(group).wait()

        @pl.when(mine != place)
        def _():
            own_copy(group, chip, mine).wait_recv()
            mate_copy(REACH, group, mine).start()

        @pl.when(has_above)
        def _():
            send_up(REACH, group, turn)

    def pass_later(slot, group, turn):
        mine = turn * CORES + core
        up_copy(slot + 1, group, mine).wait_recv()
        mate_copy(slot, group, mine).start()
        if slot > 0:

            @pl.when(has_above)
            def _():
                send_up(slot, group, turn)

    def await_mate(slot, group, turn):
        mate_copy(slot, group, turn * CORES + 1 - core).wait_recv()

    exchange_keys(0)

    @pl.loop(0, blocks)
    def _(turn):
        pass_own(0, turn)

    exchange_queries(0)
    exchange_keys(1)
    exchange_queries(1)

    log_damping = jnp.log(damp_ref[...].astype(jnp.float32)) * LOG2E
    index = lax.broadcasted_iota(jnp.int32, log_damping.shape, 0) * width
    index += lax.broadcasted_iota(jnp.int32, log_damping.shape, 1)
    first = span_ref[...]
    emphasis = (index >= first) & (index < first + SPAN)
    kept_first = jnp.minimum(first, rows - SPAN)
    kept = kept_first + lax.broadcasted_iota(jnp.int32, (1, SPAN), 1)
    kept_emphasis = (kept >= first) & (kept < first + SPAN)
    for head in range(heads):
        steered = jnp.max(
            jnp.where(steer_ref[...] == chip * heads + head, 1.0, 0.0), axis=1, keepdims=True
        )
        inside = jnp.where(emphasis, 0.0, log_damping * steered)
        beyond = jnp.where(emphasis, (1.0 - steered) * HIDDEN, HIDDEN)
        bias[0, head] = inside
        bias[1, head] = beyond
        span_bias[head] = jnp.where(kept_emphasis, (1.0 - steered) * HIDDEN, HIDDEN)

    @pl.when(plane == REACH)
    def _():
        for part in range(blocks):
            wanted = kept_first + lax.broadcasted_iota(jnp.int32, (SPAN, BLOCK), 0)
            key = lax.broadcasted_iota(jnp.int32, (SPAN, BLOCK), 1) + part * BLOCK
            pick[part] = jnp.where(wanted == key, 1.0, 0.0).astype(pick.dtype)

    acc[...] = jnp.zeros_like(acc)

    ones = jnp.ones((BLOCK, width), jnp.bfloat16)
    gap = lax.broadcasted_iota(jnp.int32, (BLOCK, BLOCK), 1) - lax.broadcasted_iota(
        jnp.int32, (BLOCK, BLOCK), 0
    )

    def add(group, turns, k, v, bias_row):
        both = jnp.concatenate([v, ones], axis=1)
        for turn in turns:
            here = pl.ds(pl.multiple_of(turn * BLOCK, BLOCK), BLOCK)
            for member in range(share):
                head = group * share + member
                raw = dot_t(q_ref[head, here, :], k)
                capped = jnp.tanh(raw * (SCORE_SCALE / SOFTCAP)) * (SOFTCAP * LOG2E)
                weight = jnp.exp2(capped + bias_row(head)).astype(jnp.bfloat16)
                acc[head, here, :] += jnp.dot(weight, both, preferred_element_type=jnp.float32)

    def add_block(group, turns, slot, key_block, bias_row):
        there = pl.ds(pl.multiple_of(slot * rows + key_block * BLOCK, BLOCK), BLOCK)
        add(group, turns, kv_ref[group, 0, there, :], kv_ref[group, 1, there, :], bias_row)

    def finish(group):
        @pl.when(plane == REACH + 1)
        def _():
            span_up(group).wait_recv()
            span_over(group, core).start()
            span_over(group, 1 - core).wait_recv()
            add(
                group, range(held), span_dst[group, 0], span_dst[group, 1],
                lambda head: span_bias[head],
            )

        @pl.loop(0, held)
        def _(turn):
            here = pl.ds(pl.multiple_of(turn * BLOCK, BLOCK), BLOCK)
            for member in range(share):
                head = group * share + member
                total = acc[head, here, :]
                done[head, here, :] = (total[:, :width] / total[:, width:]).astype(done.dtype)
            for part in range(per_block):
                at = block_of(turn) * per_block + part

                @pl.when(at == place)
                def _():
                    out_own(group).start()

                @pl.when(at != place)
                def _():
                    out_copy(group, at, chip).start()

    def global_block(slot, key_block):
        return (plane - REACH + slot) * blocks + key_block

    def bias_of(kind, head, where):
        count = BLOCK // width
        return jnp.concatenate(
            [bias[kind, head, pl.ds(where * count + part, 1), :] for part in range(count)], axis=1
        )

    def await_queries(group):
        @pl.loop(0, held * per_block)
        def _(n):
            at = block_of(n // per_block) * per_block + lax.rem(n, per_block)

            @pl.when(at == place)
            def _():
                q_own(group).wait()

            @pl.when(at != place)
            def _():
                q_copy(group, chip, at).wait_recv()

        @pl.when(group + 2 < groups)
        def _():
            exchange_keys(group + 2)
            exchange_queries(group + 2)

    def same_plane(group, key_block):
        await_mate(REACH, group, key_block)
        where = global_block(REACH, key_block)

        @pl.loop(0, held)
        def _(turn):
            @pl.when(block_of(turn) == key_block)
            def _():
                add_block(
                    group, [turn], REACH, key_block,
                    lambda head: jnp.where(gap <= 0, bias_of(0, head, where), HIDDEN),
                )

            @pl.when(block_of(turn) > key_block)
            def _():
                add_block(group, [turn], REACH, key_block, lambda head: bias_of(0, head, where))

    def next_plane(group, key_block):
        await_mate(REACH - 1, group, key_block)
        where = global_block(REACH - 1, key_block)
        add_block(group, range(held), REACH - 1, key_block, lambda head: bias_of(0, head, where))

    def hand_on(group):
        picked = jnp.zeros((SPAN, width), jnp.float32)
        for part in range(blocks):
            picked += jnp.dot(
                pick[part],
                kv_ref[group, core, part * BLOCK : (part + 1) * BLOCK, :],
                preferred_element_type=jnp.float32,
            )
        span_src[group] = picked.astype(jnp.bfloat16)
        span_up(group).start()

    def far_plane(group, key_block):
        await_mate(0, group, key_block)

        pl.when((plane == REACH) & (key_block == blocks - 1))(functools.partial(hand_on, group))

        where = global_block(0, key_block)

        @pl.loop(0, held)
        def _(turn):
            row_block = block_of(turn)

            @pl.when(row_block == key_block)
            def _():
                add_block(
                    group, [turn], 0, key_block,
                    lambda head: jnp.where(gap > 0, bias_of(0, head, where), bias_of(1, head, where)),
                )

            @pl.when(row_block != key_block)
            def _():
                beyond = (row_block + blocks - key_block) // blocks
                add_block(group, [turn], 0, key_block, lambda head: bias_of(beyond, head, where))

    far = plane // REACH
    late = jnp.maximum(plane - 1, 0)

    @pl.loop(0, groups + REACH)
    def _(round_):
        fresh = round_ < groups

        @pl.when(fresh)
        def _():
            await_queries(round_)

        @pl.loop(0, blocks)
        def _(key_block):
            @pl.when(fresh)
            def _():
                @pl.when(has_below)
                def _():
                    pass_later(REACH - 1, round_, key_block)

            @pl.when((far > 0) & (round_ > 0) & (round_ <= groups))
            def _():
                pass_later(0, round_ - 1, key_block)

            @pl.when(fresh)
            def _():
                same_plane(round_, key_block)

                @pl.when(has_below)
                def _():
                    next_plane(round_, key_block)

            @pl.when(round_ + 1 < groups)
            def _():
                pass_own(round_ + 1, key_block)

            @pl.when((far > 0) & (round_ > 0) & (round_ <= groups))
            def _():
                far_plane(round_ - 1, key_block)

        group = round_ - late
        pl.when((group >= 0) & (group < groups))(functools.partial(finish, group))

    @pl.when(has_above)
    def _():
        @pl.loop(chips - WAITING, chips)
        def _(turn):
            up_copy(REACH, groups - 1, turn * CORES + core).wait_send()

            @pl.when(has_below)
            def _():
                up_copy(REACH - 1, groups - 1, turn * CORES + core).wait_send()

    @pl.loop(0, groups)
    def _(group):
        @pl.loop(1, chips)
        def _(step):
            other = lax.rem(chip + step, chips)
            own_copy(group, other, place).wait_send()
            q_copy(group, other, place).wait_send()
            out_copy(group, place, other).wait_recv()

        @pl.when(q_owner != core)
        def _():
            q_copy(group, chip, place).wait_send()
            out_copy(group, place, chip).wait_recv()

        @pl.when(q_owner == core)
        def _():
            out_own(group).wait()

        @pl.loop(0, held * per_block)
        def _(n):
            at = block_of(n // per_block) * per_block + lax.rem(n, per_block)

            @pl.when(at != place)
            def _():
                out_copy(group, at, chip).wait_send()

        @pl.loop(0, chips)
        def _(n):
            at = n * CORES + core
            mate_copy(REACH, group, at).wait_send()

            @pl.when(has_below)
            def _():
                mate_copy(REACH - 1, group, at).wait_send()

            @pl.when(plane >= REACH)
            def _():
                mate_copy(0, group, at).wait_send()

        @pl.when(plane == REACH)
        def _():
            span_up(group).wait_send()

        @pl.when(plane == REACH + 1)
        def _():
            span_over(group, core).wait_send()


def per_device(queries, key_value, damping, span_start, steered_heads):
    chunk, head_count, width = queries.shape
    key_heads = key_value.shape[2]
    total_rows = damping.shape[0]
    devices = lax.axis_size("seq")
    plane_size = WINDOW // REACH // chunk
    planes = devices // plane_size
    rows = plane_size * chunk
    held_rows = rows // CORES
    chips = plane_size // CORES
    heads = head_count // chips
    groups = key_heads // chips
    pairs = heads * held_rows * WINDOW
    dma = pltpu.SemaphoreType.DMA
    moved = pl.pallas_call(
        functools.partial(attend, plane_size, planes),
        out_shape=jax.ShapeDtypeStruct((head_count, chunk, width), jnp.bfloat16),
        in_specs=[pl.BlockSpec(memory_space=pltpu.VMEM)] * 3 + [pl.BlockSpec(memory_space=pl.ANY)] * 2,
        out_specs=pl.BlockSpec(memory_space=pl.ANY),
        scratch_shapes=[
            pltpu.VMEM((heads, held_rows, width), jnp.bfloat16),
            pltpu.VMEM((groups, 2, (REACH + 1) * rows, width), jnp.bfloat16),
            pltpu.VMEM((groups, SPAN, width), jnp.bfloat16),
            pltpu.VMEM((groups, 2, SPAN, width), jnp.bfloat16),
            pltpu.VMEM((heads, held_rows, 2 * width), jnp.float32),
            pltpu.VMEM((heads, held_rows, width), jnp.bfloat16),
            pltpu.VMEM((2, heads, total_rows // width, width), jnp.float32),
            pltpu.VMEM((heads, 1, SPAN), jnp.float32),
            pltpu.VMEM((rows // BLOCK, SPAN, BLOCK), jnp.bfloat16),
            dma((groups, chips)),
            dma((groups, plane_size)),
            dma((groups, chips)),
            dma((REACH + 1, groups, plane_size)),
            dma((REACH, groups, plane_size)),
            dma((REACH + 1, groups, plane_size)),
            dma((groups,)),
            dma((groups,)),
            dma((groups, 2)),
            dma((groups, plane_size)),
            dma((groups, chips)),
        ],
        compiler_params=pltpu.CompilerParams(
            collective_id=0, has_side_effects=True, vmem_limit_bytes=36 * 1024 * 1024
        ),
        cost_estimate=pl.CostEstimate(
            flops=6 * pairs * width,
            transcendentals=2 * pairs,
            bytes_accessed=6 * chunk * head_count * width,
        ),
        name="attend",
    )(
        span_start.reshape(1, 1),
        steered_heads.reshape(1, -1),
        damping.reshape(-1, width),
        queries.transpose(1, 0, 2),
        key_value.transpose(2, 0, 1, 3),
    )
    return moved.transpose(1, 0, 2)


def solution(mesh):
    in_specs = (
        P(("prompt", "seq"), None, None),
        P(None, ("prompt", "seq"), None, None),
        P("prompt"),
        P("prompt"),
        P(),
    )
    out_specs = P(("prompt", "seq"), None, None)
    return jax.shard_map(
        per_device, mesh=mesh, in_specs=in_specs, out_specs=out_specs, check_vma=False
    )
```

```python
import functools

import jax
import jax.numpy as jnp
from jax import lax
from jax.experimental import pallas as pl
from jax.experimental.pallas import tpu as pltpu
from jax.sharding import PartitionSpec as P

WINDOW = 4096
SPAN = 512
SCORE_SCALE = 144.0 ** (-0.5)
SOFTCAP = 50.0
LOG2E = 1.4426950408889634
BLOCK = 512
REACH = 2
CORES = 2
WAITING = 4
HIDDEN = -1e30
MESH = pl.DeviceIdType.MESH


def dot_t(q, k):
    return lax.dot_general(q, k, (((1,), (1,)), ((), ())), preferred_element_type=jnp.float32)


def attend(
    plane_size, planes,
    span_ref, steer_ref, damp_ref, q_in, kv_in, out_ref,
    q_ref, kv_ref, span_src, span_dst, acc, done, bias, span_bias, pick,
    q_send, q_recv, own_send, mate_send, up_send, kv_recv,
    span_send, span_mate, span_recv, out_send, out_recv,
):
    me = lax.axis_index("seq")
    plane = me // plane_size
    place = lax.rem(me, plane_size)
    chip, core = place // CORES, lax.rem(place, CORES)
    chips = plane_size // CORES
    chunk = q_in.shape[1]
    rows = plane_size * chunk
    blocks = rows // BLOCK
    per_block = BLOCK // chunk
    held = blocks // CORES
    heads, _, width = q_ref.shape
    groups = kv_ref.shape[0]
    share = heads // groups
    has_below = plane > 0
    has_above = plane < planes - 1

    def block_of(turn):
        return core + turn * (blocks - 1 - 2 * core)

    def owner(row_block):
        return lax.rem((row_block + 1) // 2, CORES)

    def held_rows(at):
        return pl.ds(at // per_block // CORES * BLOCK + lax.rem(at, per_block) * chunk, chunk)

    def at_place(other):
        return {"seq": plane * plane_size + other}

    mate = at_place(chip * CORES + 1 - core)
    above = {"seq": me + plane_size}

    def remote(source, target, send_sem, recv_sem, device):
        return pltpu.make_async_remote_copy(
            src_ref=source,
            dst_ref=target,
            send_sem=send_sem,
            recv_sem=recv_sem,
            device_id=device,
            device_id_type=MESH,
        )

    def of_group(group):
        return pl.ds(group * share, share)

    def q_source(group, other):
        return q_in.at[pl.ds(other * heads + group * share, share)]

    def q_copy(group, other, at):
        return remote(
            q_source(group, other),
            q_ref.at[of_group(group), held_rows(at)],
            q_send.at[group, other],
            q_recv.at[group, at],
            at_place(other * CORES + owner(at // per_block)),
        )

    def q_own(group):
        return pltpu.make_async_copy(
            q_source(group, chip),
            q_ref.at[of_group(group), held_rows(place)],
            q_recv.at[group, place],
        )

    def keys_at(slot, group, at):
        return kv_ref.at[group, :, pl.ds(slot * rows + at * chunk, chunk)]

    def own_copy(group, other, at):
        return remote(
            kv_in.at[other * groups + group],
            keys_at(REACH, group, at),
            own_send.at[group, other],
            kv_recv.at[REACH, group, at],
            at_place(other * CORES + core),
        )

    def own_local(group):
        return pltpu.make_async_copy(
            kv_in.at[chip * groups + group],
            keys_at(REACH, group, place),
            kv_recv.at[REACH, group, place],
        )

    def mate_copy(slot, group, at, source=None):
        return remote(
            keys_at(slot, group, at) if source is None else source,
            keys_at(slot, group, at),
            mate_send.at[slot, group, at],
            kv_recv.at[slot, group, at],
            mate,
        )

    def up_copy(slot, group, at, source=None):
        return remote(
            keys_at(slot, group, at) if source is None else source,
            keys_at(slot - 1, group, at),
            up_send.at[slot - 1, group, at],
            kv_recv.at[slot - 1, group, at],
            above,
        )

    def span_up(group):
        return remote(
            span_src.at[group],
            span_dst.at[group, core],
            span_send.at[group],
            span_recv.at[group, core],
            above,
        )

    def span_over(group, half):
        return remote(
            span_dst.at[group, half],
            span_dst.at[group, half],
            span_mate.at[group],
            span_recv.at[group, half],
            mate,
        )

    def out_copy(group, at, sender):
        return remote(
            done.at[of_group(group), held_rows(at)],
            out_ref.at[pl.ds(sender * heads + group * share, share)],
            out_send.at[group, at],
            out_recv.at[group, sender],
            at_place(at),
        )

    def out_own(group):
        return pltpu.make_async_copy(
            done.at[of_group(group), held_rows(place)],
            out_ref.at[pl.ds(chip * heads + group * share, share)],
            out_recv.at[group, chip],
        )

    barrier = pltpu.get_barrier_semaphore()

    def greet(device):
        pl.semaphore_signal(barrier, inc=1, device_id=device, device_id_type=MESH)

    @pl.loop(1, plane_size)
    def _(step):
        greet(at_place(lax.rem(place + step, plane_size)))

    @pl.when(has_below)
    def _():
        greet({"seq": me - plane_size})

    @pl.when(has_above)
    def _():
        greet(above)

    neighbours = (plane + planes - 1) // planes + (2 * planes - 2 - plane) // planes
    pl.semaphore_wait(barrier, plane_size - 1 + neighbours)

    q_owner = owner(place // per_block)

    def exchange_keys(group):
        @pl.loop(1, chips)
        def _(step):
            own_copy(group, lax.rem(chip + step, chips), place).start()

        own_local(group).start()
        mate_copy(REACH, group, place, kv_in.at[chip * groups + group]).start()

    def exchange_queries(group):
        @pl.loop(1, chips)
        def _(step):
            q_copy(group, lax.rem(chip + step, chips), place).start()

        @pl.when(q_owner == core)
        def _():
            q_own(group).start()

        @pl.when(q_owner != core)
        def _():
            q_copy(group, chip, place).start()

    def send_up(slot, group, turn):
        @pl.when(turn >= WAITING)
        def _():
            up_copy(slot, group, (turn - WAITING) * CORES + core).wait_send()

        @pl.when((turn < WAITING) & (group > 0))
        def _():
            earlier = turn + chips - WAITING
            up_copy(slot, group - 1, earlier * CORES + core).wait_send()

        up_copy(slot, group, turn * CORES + core).start()

    def pass_own(group, turn):
        mine = turn * CORES + core

        @pl.when(mine == place)
        def _():
            own_local(group).wait()

        @pl.when(mine != place)
        def _():
            own_copy(group, chip, mine).wait_recv()
            mate_copy(REACH, group, mine).start()

        @pl.when(has_above)
        def _():
            send_up(REACH, group, turn)

    def pass_later(slot, group, turn):
        mine = turn * CORES + core
        up_copy(slot + 1, group, mine).wait_recv()
        mate_copy(slot, group, mine).start()
        if slot > 0:

            @pl.when(has_above)
            def _():
                send_up(slot, group, turn)

    def await_mate(slot, group, turn):
        mate_copy(slot, group, turn * CORES + 1 - core).wait_recv()

    exchange_keys(0)

    @pl.loop(0, chips)
    def _(step):
        pass_own(0, lax.rem(chip + chips - step, chips))

    exchange_queries(0)
    exchange_keys(1)
    exchange_queries(1)

    log_damping = jnp.log(damp_ref[...].astype(jnp.float32)) * LOG2E
    index = lax.broadcasted_iota(jnp.int32, log_damping.shape, 0) * width
    index += lax.broadcasted_iota(jnp.int32, log_damping.shape, 1)
    first = span_ref[...]
    emphasis = (index >= first) & (index < first + SPAN)
    kept_first = jnp.minimum(first, rows - SPAN)
    kept = kept_first + lax.broadcasted_iota(jnp.int32, (1, SPAN), 1)
    kept_emphasis = (kept >= first) & (kept < first + SPAN)
    for head in range(heads):
        steered = jnp.max(
            jnp.where(steer_ref[...] == chip * heads + head, 1.0, 0.0), axis=1, keepdims=True
        )
        inside = jnp.where(emphasis, 0.0, log_damping * steered)
        beyond = jnp.where(emphasis, (1.0 - steered) * HIDDEN, HIDDEN)
        bias[0, head] = inside
        bias[1, head] = beyond
        span_bias[head] = jnp.where(kept_emphasis, (1.0 - steered) * HIDDEN, HIDDEN)

    @pl.when(plane == REACH)
    def _():
        for part in range(blocks):
            wanted = kept_first + lax.broadcasted_iota(jnp.int32, (SPAN, BLOCK), 0)
            key = lax.broadcasted_iota(jnp.int32, (SPAN, BLOCK), 1) + part * BLOCK
            pick[part] = jnp.where(wanted == key, 1.0, 0.0).astype(pick.dtype)

    acc[...] = jnp.zeros_like(acc)

    ones = jnp.ones((BLOCK, width), jnp.bfloat16)
    gap = lax.broadcasted_iota(jnp.int32, (BLOCK, BLOCK), 1) - lax.broadcasted_iota(
        jnp.int32, (BLOCK, BLOCK), 0
    )

    def add(group, turns, k, v, bias_row):
        both = jnp.concatenate([v, ones], axis=1)
        for turn in turns:
            here = pl.ds(pl.multiple_of(turn * BLOCK, BLOCK), BLOCK)
            for member in range(share):
                head = group * share + member
                raw = dot_t(q_ref[head, here, :], k)
                capped = jnp.tanh(raw * (SCORE_SCALE / SOFTCAP)) * (SOFTCAP * LOG2E)
                weight = jnp.exp2(capped + bias_row(head)).astype(jnp.bfloat16)
                acc[head, here, :] += jnp.dot(weight, both, preferred_element_type=jnp.float32)

    def add_block(group, turns, slot, key_block, bias_row):
        there = pl.ds(pl.multiple_of(slot * rows + key_block * BLOCK, BLOCK), BLOCK)
        add(group, turns, kv_ref[group, 0, there, :], kv_ref[group, 1, there, :], bias_row)

    def finish(group):
        @pl.when(plane == REACH + 1)
        def _():
            span_up(group).wait_recv()
            span_over(group, core).start()
            span_over(group, 1 - core).wait_recv()
            add(
                group, range(held), span_dst[group, 0], span_dst[group, 1],
                lambda head: span_bias[head],
            )

        @pl.loop(0, held)
        def _(turn):
            here = pl.ds(pl.multiple_of(turn * BLOCK, BLOCK), BLOCK)
            for member in range(share):
                head = group * share + member
                total = acc[head, here, :]
                done[head, here, :] = (total[:, :width] / total[:, width:]).astype(done.dtype)
            for part in range(per_block):
                at = block_of(turn) * per_block + part

                @pl.when(at == place)
                def _():
                    out_own(group).start()

                @pl.when(at != place)
                def _():
                    out_copy(group, at, chip).start()

    def global_block(slot, key_block):
        return (plane - REACH + slot) * blocks + key_block

    def bias_of(kind, head, where):
        count = BLOCK // width
        return jnp.concatenate(
            [bias[kind, head, pl.ds(where * count + part, 1), :] for part in range(count)], axis=1
        )

    def await_queries(group):
        @pl.loop(0, held * per_block)
        def _(n):
            at = block_of(n // per_block) * per_block + lax.rem(n, per_block)

            @pl.when(at == place)
            def _():
                q_own(group).wait()

            @pl.when(at != place)
            def _():
                q_copy(group, chip, at).wait_recv()

        @pl.when(group + 2 < groups)
        def _():
            exchange_keys(group + 2)
            exchange_queries(group + 2)

    def same_plane(group, key_block):
        await_mate(REACH, group, key_block)
        where = global_block(REACH, key_block)

        @pl.loop(0, held)
        def _(turn):
            @pl.when(block_of(turn) == key_block)
            def _():
                add_block(
                    group, [turn], REACH, key_block,
                    lambda head: jnp.where(gap <= 0, bias_of(0, head, where), HIDDEN),
                )

            @pl.when(block_of(turn) > key_block)
            def _():
                add_block(group, [turn], REACH, key_block, lambda head: bias_of(0, head, where))

    def next_plane(group, key_block):
        await_mate(REACH - 1, group, key_block)
        where = global_block(REACH - 1, key_block)
        add_block(group, range(held), REACH - 1, key_block, lambda head: bias_of(0, head, where))

    def hand_on(group):
        picked = jnp.zeros((SPAN, width), jnp.float32)
        for part in range(blocks):
            picked += jnp.dot(
                pick[part],
                kv_ref[group, core, part * BLOCK : (part + 1) * BLOCK, :],
                preferred_element_type=jnp.float32,
            )
        span_src[group] = picked.astype(jnp.bfloat16)
        span_up(group).start()

    def far_plane(group, key_block):
        await_mate(0, group, key_block)

        pl.when((plane == REACH) & (key_block == blocks - 1))(functools.partial(hand_on, group))

        where = global_block(0, key_block)

        @pl.loop(0, held)
        def _(turn):
            row_block = block_of(turn)

            @pl.when(row_block == key_block)
            def _():
                add_block(
                    group, [turn], 0, key_block,
                    lambda head: jnp.where(gap > 0, bias_of(0, head, where), bias_of(1, head, where)),
                )

            @pl.when(row_block != key_block)
            def _():
                beyond = (row_block + blocks - key_block) // blocks
                add_block(group, [turn], 0, key_block, lambda head: bias_of(beyond, head, where))

    far = plane // REACH
    late = jnp.maximum(plane - 1, 0)

    @pl.loop(0, groups + REACH)
    def _(round_):
        fresh = round_ < groups

        @pl.when(fresh)
        def _():
            await_queries(round_)

        @pl.loop(0, blocks)
        def _(key_block):
            @pl.when(fresh)
            def _():
                @pl.when(has_below)
                def _():
                    pass_later(REACH - 1, round_, key_block)

            @pl.when((far > 0) & (round_ > 0) & (round_ <= groups))
            def _():
                pass_later(0, round_ - 1, key_block)

            @pl.when(fresh)
            def _():
                same_plane(round_, key_block)

                @pl.when(has_below)
                def _():
                    next_plane(round_, key_block)

            @pl.when(round_ + 1 < groups)
            def _():
                pass_own(round_ + 1, key_block)

            @pl.when((far > 0) & (round_ > 0) & (round_ <= groups))
            def _():
                far_plane(round_ - 1, key_block)

        group = round_ - late
        pl.when((group >= 0) & (group < groups))(functools.partial(finish, group))

    @pl.when(has_above)
    def _():
        @pl.loop(chips - WAITING, chips)
        def _(turn):
            up_copy(REACH, groups - 1, turn * CORES + core).wait_send()

            @pl.when(has_below)
            def _():
                up_copy(REACH - 1, groups - 1, turn * CORES + core).wait_send()

    @pl.loop(0, groups)
    def _(group):
        @pl.loop(1, chips)
        def _(step):
            other = lax.rem(chip + step, chips)
            own_copy(group, other, place).wait_send()
            q_copy(group, other, place).wait_send()
            out_copy(group, place, other).wait_recv()

        @pl.when(q_owner != core)
        def _():
            q_copy(group, chip, place).wait_send()
            out_copy(group, place, chip).wait_recv()

        @pl.when(q_owner == core)
        def _():
            out_own(group).wait()

        @pl.loop(0, held * per_block)
        def _(n):
            at = block_of(n // per_block) * per_block + lax.rem(n, per_block)

            @pl.when(at != place)
            def _():
                out_copy(group, at, chip).wait_send()

        @pl.loop(0, chips)
        def _(n):
            at = n * CORES + core
            mate_copy(REACH, group, at).wait_send()

            @pl.when(has_below)
            def _():
                mate_copy(REACH - 1, group, at).wait_send()

            @pl.when(plane >= REACH)
            def _():
                mate_copy(0, group, at).wait_send()

        @pl.when(plane == REACH)
        def _():
            span_up(group).wait_send()

        @pl.when(plane == REACH + 1)
        def _():
            span_over(group, core).wait_send()


def per_device(queries, key_value, damping, span_start, steered_heads):
    chunk, head_count, width = queries.shape
    key_heads = key_value.shape[2]
    total_rows = damping.shape[0]
    devices = lax.axis_size("seq")
    plane_size = WINDOW // REACH // chunk
    planes = devices // plane_size
    rows = plane_size * chunk
    held_rows = rows // CORES
    chips = plane_size // CORES
    heads = head_count // chips
    groups = key_heads // chips
    pairs = heads * held_rows * WINDOW
    dma = pltpu.SemaphoreType.DMA
    moved = pl.pallas_call(
        functools.partial(attend, plane_size, planes),
        out_shape=jax.ShapeDtypeStruct((head_count, chunk, width), jnp.bfloat16),
        in_specs=[pl.BlockSpec(memory_space=pltpu.VMEM)] * 3 + [pl.BlockSpec(memory_space=pl.ANY)] * 2,
        out_specs=pl.BlockSpec(memory_space=pl.ANY),
        scratch_shapes=[
            pltpu.VMEM((heads, held_rows, width), jnp.bfloat16),
            pltpu.VMEM((groups, 2, (REACH + 1) * rows, width), jnp.bfloat16),
            pltpu.VMEM((groups, SPAN, width), jnp.bfloat16),
            pltpu.VMEM((groups, 2, SPAN, width), jnp.bfloat16),
            pltpu.VMEM((heads, held_rows, 2 * width), jnp.float32),
            pltpu.VMEM((heads, held_rows, width), jnp.bfloat16),
            pltpu.VMEM((2, heads, total_rows // width, width), jnp.float32),
            pltpu.VMEM((heads, 1, SPAN), jnp.float32),
            pltpu.VMEM((rows // BLOCK, SPAN, BLOCK), jnp.bfloat16),
            dma((groups, chips)),
            dma((groups, plane_size)),
            dma((groups, chips)),
            dma((REACH + 1, groups, plane_size)),
            dma((REACH, groups, plane_size)),
            dma((REACH + 1, groups, plane_size)),
            dma((groups,)),
            dma((groups,)),
            dma((groups, 2)),
            dma((groups, plane_size)),
            dma((groups, chips)),
        ],
        compiler_params=pltpu.CompilerParams(
            collective_id=0, has_side_effects=True, vmem_limit_bytes=36 * 1024 * 1024
        ),
        cost_estimate=pl.CostEstimate(
            flops=6 * pairs * width,
            transcendentals=2 * pairs,
            bytes_accessed=6 * chunk * head_count * width,
        ),
        name="attend",
    )(
        span_start.reshape(1, 1),
        steered_heads.reshape(1, -1),
        damping.reshape(-1, width),
        queries.transpose(1, 0, 2),
        key_value.transpose(2, 0, 1, 3),
    )
    return moved.transpose(1, 0, 2)


def solution(mesh):
    in_specs = (
        P(("prompt", "seq"), None, None),
        P(None, ("prompt", "seq"), None, None),
        P("prompt"),
        P("prompt"),
        P(),
    )
    out_specs = P(("prompt", "seq"), None, None)
    return jax.shard_map(
        per_device, mesh=mesh, in_specs=in_specs, out_specs=out_specs, check_vma=False
    )
```

```python
import functools

import jax
import jax.numpy as jnp
from jax import lax
from jax.experimental import pallas as pl
from jax.experimental.pallas import tpu as pltpu
from jax.sharding import PartitionSpec as P

WINDOW = 4096
SPAN = 512
SCORE_SCALE = 144.0 ** (-0.5)
SOFTCAP = 50.0
LOG2E = 1.4426950408889634
BLOCK = 512
REACH = 2
CORES = 2
WAITING = 4
HIDDEN = -1e30
MESH = pl.DeviceIdType.MESH


def dot_t(q, k):
    return lax.dot_general(q, k, (((1,), (1,)), ((), ())), preferred_element_type=jnp.float32)


def attend(
    plane_size, planes,
    span_ref, steer_ref, damp_ref, q_in, kv_in, out_ref,
    q_ref, kv_ref, span_src, span_dst, acc, done, bias, span_bias, pick,
    q_send, q_recv, own_send, mate_send, up_send, kv_recv,
    span_send, span_mate, span_recv, out_send, out_recv,
):
    me = lax.axis_index("seq")
    plane = me // plane_size
    place = lax.rem(me, plane_size)
    chip, core = place // CORES, lax.rem(place, CORES)
    chips = plane_size // CORES
    chunk = q_in.shape[1]
    rows = plane_size * chunk
    blocks = rows // BLOCK
    per_block = BLOCK // chunk
    held = blocks // CORES
    heads, _, width = q_ref.shape
    groups = kv_ref.shape[0]
    share = heads // groups
    has_below = plane > 0
    has_above = plane < planes - 1

    def block_of(turn):
        return core + turn * (blocks - 1 - 2 * core)

    def owner(row_block):
        return lax.rem((row_block + 1) // 2, CORES)

    def held_rows(at):
        return pl.ds(at // per_block // CORES * BLOCK + lax.rem(at, per_block) * chunk, chunk)

    def at_place(other):
        return {"seq": plane * plane_size + other}

    mate = at_place(chip * CORES + 1 - core)
    above = {"seq": me + plane_size}

    def remote(source, target, send_sem, recv_sem, device):
        return pltpu.make_async_remote_copy(
            src_ref=source,
            dst_ref=target,
            send_sem=send_sem,
            recv_sem=recv_sem,
            device_id=device,
            device_id_type=MESH,
        )

    def of_group(group):
        return pl.ds(group * share, share)

    def q_source(group, other):
        return q_in.at[pl.ds(other * heads + group * share, share)]

    def q_copy(group, other, at):
        return remote(
            q_source(group, other),
            q_ref.at[of_group(group), held_rows(at)],
            q_send.at[group, other],
            q_recv.at[group, at],
            at_place(other * CORES + owner(at // per_block)),
        )

    def q_own(group):
        return pltpu.make_async_copy(
            q_source(group, chip),
            q_ref.at[of_group(group), held_rows(place)],
            q_recv.at[group, place],
        )

    def keys_at(slot, group, at):
        return kv_ref.at[group, :, pl.ds(slot * rows + at * chunk, chunk)]

    def own_copy(group, other, at):
        return remote(
            kv_in.at[other * groups + group],
            keys_at(REACH, group, at),
            own_send.at[group, other],
            kv_recv.at[REACH, group, at],
            at_place(other * CORES + core),
        )

    def own_local(group):
        return pltpu.make_async_copy(
            kv_in.at[chip * groups + group],
            keys_at(REACH, group, place),
            kv_recv.at[REACH, group, place],
        )

    def mate_copy(slot, group, at, source=None):
        return remote(
            keys_at(slot, group, at) if source is None else source,
            keys_at(slot, group, at),
            mate_send.at[slot, group, at],
            kv_recv.at[slot, group, at],
            mate,
        )

    def up_copy(slot, group, at, source=None):
        return remote(
            keys_at(slot, group, at) if source is None else source,
            keys_at(slot - 1, group, at),
            up_send.at[slot - 1, group, at],
            kv_recv.at[slot - 1, group, at],
            above,
        )

    def span_up(group):
        return remote(
            span_src.at[group],
            span_dst.at[group, core],
            span_send.at[group],
            span_recv.at[group, core],
            above,
        )

    def span_over(group, half):
        return remote(
            span_dst.at[group, half],
            span_dst.at[group, half],
            span_mate.at[group],
            span_recv.at[group, half],
            mate,
        )

    def out_copy(group, at, sender):
        return remote(
            done.at[of_group(group), held_rows(at)],
            out_ref.at[pl.ds(sender * heads + group * share, share)],
            out_send.at[group, at],
            out_recv.at[group, sender],
            at_place(at),
        )

    def out_own(group):
        return pltpu.make_async_copy(
            done.at[of_group(group), held_rows(place)],
            out_ref.at[pl.ds(chip * heads + group * share, share)],
            out_recv.at[group, chip],
        )

    barrier = pltpu.get_barrier_semaphore()

    def greet(device):
        pl.semaphore_signal(barrier, inc=1, device_id=device, device_id_type=MESH)

    @pl.loop(1, plane_size)
    def _(step):
        greet(at_place(lax.rem(place + step, plane_size)))

    @pl.when(has_below)
    def _():
        greet({"seq": me - plane_size})

    @pl.when(has_above)
    def _():
        greet(above)

    neighbours = (plane + planes - 1) // planes + (2 * planes - 2 - plane) // planes
    pl.semaphore_wait(barrier, plane_size - 1 + neighbours)

    q_owner = owner(place // per_block)

    def exchange_keys(group):
        @pl.loop(1, chips)
        def _(step):
            own_copy(group, lax.rem(chip + step, chips), place).start()

        own_local(group).start()
        mate_copy(REACH, group, place, kv_in.at[chip * groups + group]).start()

    def exchange_queries(group):
        @pl.loop(1, chips)
        def _(step):
            q_copy(group, lax.rem(chip + step, chips), place).start()

        @pl.when(q_owner == core)
        def _():
            q_own(group).start()

        @pl.when(q_owner != core)
        def _():
            q_copy(group, chip, place).start()

    def send_up(slot, group, turn):
        @pl.when(turn >= WAITING)
        def _():
            up_copy(slot, group, (turn - WAITING) * CORES + core).wait_send()

        @pl.when((turn < WAITING) & (group > 0))
        def _():
            earlier = turn + chips - WAITING
            up_copy(slot, group - 1, earlier * CORES + core).wait_send()

        up_copy(slot, group, turn * CORES + core).start()

    def pass_own(group, turn):
        mine = turn * CORES + core

        @pl.when(mine == place)
        def _():
            own_local(group).wait()

        @pl.when(mine != place)
        def _():
            own_copy(group, chip, mine).wait_recv()
            mate_copy(REACH, group, mine).start()

        @pl.when(has_above & ((group > 0) | (mine != place)))
        def _():
            send_up(REACH, group, turn)

    def pass_later(slot, group, turn):
        mine = turn * CORES + core
        up_copy(slot + 1, group, mine).wait_recv()
        mate_copy(slot, group, mine).start()
        if slot > 0:

            @pl.when(has_above)
            def _():
                send_up(slot, group, turn)

    def await_mate(slot, group, turn):
        mate_copy(slot, group, turn * CORES + 1 - core).wait_recv()

    @pl.when(has_above)
    def _():
        up_copy(REACH, 0, place, kv_in.at[chip * groups]).start()

    exchange_keys(0)

    @pl.loop(0, chips)
    def _(step):
        pass_own(0, lax.rem(chip + chips - step, chips))

    exchange_queries(0)
    exchange_keys(1)
    exchange_queries(1)

    log_damping = jnp.log(damp_ref[...].astype(jnp.float32)) * LOG2E
    index = lax.broadcasted_iota(jnp.int32, log_damping.shape, 0) * width
    index += lax.broadcasted_iota(jnp.int32, log_damping.shape, 1)
    first = span_ref[...]
    emphasis = (index >= first) & (index < first + SPAN)
    kept_first = jnp.minimum(first, rows - SPAN)
    kept = kept_first + lax.broadcasted_iota(jnp.int32, (1, SPAN), 1)
    kept_emphasis = (kept >= first) & (kept < first + SPAN)
    for head in range(heads):
        steered = jnp.max(
            jnp.where(steer_ref[...] == chip * heads + head, 1.0, 0.0), axis=1, keepdims=True
        )
        inside = jnp.where(emphasis, 0.0, log_damping * steered)
        beyond = jnp.where(emphasis, (1.0 - steered) * HIDDEN, HIDDEN)
        bias[0, head] = inside
        bias[1, head] = beyond
        span_bias[head] = jnp.where(kept_emphasis, (1.0 - steered) * HIDDEN, HIDDEN)

    @pl.when(plane == REACH)
    def _():
        for part in range(blocks):
            wanted = kept_first + lax.broadcasted_iota(jnp.int32, (SPAN, BLOCK), 0)
            key = lax.broadcasted_iota(jnp.int32, (SPAN, BLOCK), 1) + part * BLOCK
            pick[part] = jnp.where(wanted == key, 1.0, 0.0).astype(pick.dtype)

    acc[...] = jnp.zeros_like(acc)

    ones = jnp.ones((BLOCK, width), jnp.bfloat16)
    gap = lax.broadcasted_iota(jnp.int32, (BLOCK, BLOCK), 1) - lax.broadcasted_iota(
        jnp.int32, (BLOCK, BLOCK), 0
    )

    def add(group, turns, k, v, bias_row):
        both = jnp.concatenate([v, ones], axis=1)
        for turn in turns:
            here = pl.ds(pl.multiple_of(turn * BLOCK, BLOCK), BLOCK)
            for member in range(share):
                head = group * share + member
                raw = dot_t(q_ref[head, here, :], k)
                capped = jnp.tanh(raw * (SCORE_SCALE / SOFTCAP)) * (SOFTCAP * LOG2E)
                weight = jnp.exp2(capped + bias_row(head)).astype(jnp.bfloat16)
                acc[head, here, :] += jnp.dot(weight, both, preferred_element_type=jnp.float32)

    def add_block(group, turns, slot, key_block, bias_row):
        there = pl.ds(pl.multiple_of(slot * rows + key_block * BLOCK, BLOCK), BLOCK)
        add(group, turns, kv_ref[group, 0, there, :], kv_ref[group, 1, there, :], bias_row)

    def finish(group):
        @pl.when(plane == REACH + 1)
        def _():
            span_up(group).wait_recv()
            span_over(group, core).start()
            span_over(group, 1 - core).wait_recv()
            add(
                group, range(held), span_dst[group, 0], span_dst[group, 1],
                lambda head: span_bias[head],
            )

        @pl.loop(0, held)
        def _(turn):
            here = pl.ds(pl.multiple_of(turn * BLOCK, BLOCK), BLOCK)
            for member in range(share):
                head = group * share + member
                total = acc[head, here, :]
                done[head, here, :] = (total[:, :width] / total[:, width:]).astype(done.dtype)
            for part in range(per_block):
                at = block_of(turn) * per_block + part

                @pl.when(at == place)
                def _():
                    out_own(group).start()

                @pl.when(at != place)
                def _():
                    out_copy(group, at, chip).start()

    def global_block(slot, key_block):
        return (plane - REACH + slot) * blocks + key_block

    def bias_of(kind, head, where):
        count = BLOCK // width
        return jnp.concatenate(
            [bias[kind, head, pl.ds(where * count + part, 1), :] for part in range(count)], axis=1
        )

    def await_queries(group):
        @pl.loop(0, held * per_block)
        def _(n):
            at = block_of(n // per_block) * per_block + lax.rem(n, per_block)

            @pl.when(at == place)
            def _():
                q_own(group).wait()

            @pl.when(at != place)
            def _():
                q_copy(group, chip, at).wait_recv()

        @pl.when(group + 2 < groups)
        def _():
            exchange_keys(group + 2)
            exchange_queries(group + 2)

    def same_plane(group, key_block):
        await_mate(REACH, group, key_block)
        where = global_block(REACH, key_block)

        @pl.loop(0, held)
        def _(turn):
            @pl.when(block_of(turn) == key_block)
            def _():
                add_block(
                    group, [turn], REACH, key_block,
                    lambda head: jnp.where(gap <= 0, bias_of(0, head, where), HIDDEN),
                )

            @pl.when(block_of(turn) > key_block)
            def _():
                add_block(group, [turn], REACH, key_block, lambda head: bias_of(0, head, where))

    def next_plane(group, key_block):
        await_mate(REACH - 1, group, key_block)
        where = global_block(REACH - 1, key_block)
        add_block(group, range(held), REACH - 1, key_block, lambda head: bias_of(0, head, where))

    def hand_on(group):
        picked = jnp.zeros((SPAN, width), jnp.float32)
        for part in range(blocks):
            picked += jnp.dot(
                pick[part],
                kv_ref[group, core, part * BLOCK : (part + 1) * BLOCK, :],
                preferred_element_type=jnp.float32,
            )
        span_src[group] = picked.astype(jnp.bfloat16)
        span_up(group).start()

    def far_plane(group, key_block):
        await_mate(0, group, key_block)

        pl.when((plane == REACH) & (key_block == blocks - 1))(functools.partial(hand_on, group))

        where = global_block(0, key_block)

        @pl.loop(0, held)
        def _(turn):
            row_block = block_of(turn)

            @pl.when(row_block == key_block)
            def _():
                add_block(
                    group, [turn], 0, key_block,
                    lambda head: jnp.where(gap > 0, bias_of(0, head, where), bias_of(1, head, where)),
                )

            @pl.when(row_block != key_block)
            def _():
                beyond = (row_block + blocks - key_block) // blocks
                add_block(group, [turn], 0, key_block, lambda head: bias_of(beyond, head, where))

    far = plane // REACH
    late = jnp.maximum(plane - 1, 0)

    @pl.loop(0, groups + REACH)
    def _(round_):
        fresh = round_ < groups

        @pl.when(fresh)
        def _():
            await_queries(round_)

        @pl.loop(0, blocks)
        def _(key_block):
            @pl.when(fresh)
            def _():
                @pl.when(has_below)
                def _():
                    pass_later(REACH - 1, round_, key_block)

            @pl.when((far > 0) & (round_ > 0) & (round_ <= groups))
            def _():
                pass_later(0, round_ - 1, key_block)

            @pl.when(fresh)
            def _():
                same_plane(round_, key_block)

                @pl.when(has_below)
                def _():
                    next_plane(round_, key_block)

            @pl.when(round_ + 1 < groups)
            def _():
                pass_own(round_ + 1, key_block)

            @pl.when((far > 0) & (round_ > 0) & (round_ <= groups))
            def _():
                far_plane(round_ - 1, key_block)

        group = round_ - late
        pl.when((group >= 0) & (group < groups))(functools.partial(finish, group))

    @pl.when(has_above)
    def _():
        @pl.loop(chips - WAITING, chips)
        def _(turn):
            up_copy(REACH, groups - 1, turn * CORES + core).wait_send()

            @pl.when(has_below)
            def _():
                up_copy(REACH - 1, groups - 1, turn * CORES + core).wait_send()

    @pl.loop(0, groups)
    def _(group):
        @pl.loop(1, chips)
        def _(step):
            other = lax.rem(chip + step, chips)
            own_copy(group, other, place).wait_send()
            q_copy(group, other, place).wait_send()
            out_copy(group, place, other).wait_recv()

        @pl.when(q_owner != core)
        def _():
            q_copy(group, chip, place).wait_send()
            out_copy(group, place, chip).wait_recv()

        @pl.when(q_owner == core)
        def _():
            out_own(group).wait()

        @pl.loop(0, held * per_block)
        def _(n):
            at = block_of(n // per_block) * per_block + lax.rem(n, per_block)

            @pl.when(at != place)
            def _():
                out_copy(group, at, chip).wait_send()

        @pl.loop(0, chips)
        def _(n):
            at = n * CORES + core
            mate_copy(REACH, group, at).wait_send()

            @pl.when(has_below)
            def _():
                mate_copy(REACH - 1, group, at).wait_send()

            @pl.when(plane >= REACH)
            def _():
                mate_copy(0, group, at).wait_send()

        @pl.when(plane == REACH)
        def _():
            span_up(group).wait_send()

        @pl.when(plane == REACH + 1)
        def _():
            span_over(group, core).wait_send()


def per_device(queries, key_value, damping, span_start, steered_heads):
    chunk, head_count, width = queries.shape
    key_heads = key_value.shape[2]
    total_rows = damping.shape[0]
    devices = lax.axis_size("seq")
    plane_size = WINDOW // REACH // chunk
    planes = devices // plane_size
    rows = plane_size * chunk
    held_rows = rows // CORES
    chips = plane_size // CORES
    heads = head_count // chips
    groups = key_heads // chips
    pairs = heads * held_rows * WINDOW
    dma = pltpu.SemaphoreType.DMA
    moved = pl.pallas_call(
        functools.partial(attend, plane_size, planes),
        out_shape=jax.ShapeDtypeStruct((head_count, chunk, width), jnp.bfloat16),
        in_specs=[pl.BlockSpec(memory_space=pltpu.VMEM)] * 3 + [pl.BlockSpec(memory_space=pl.ANY)] * 2,
        out_specs=pl.BlockSpec(memory_space=pl.ANY),
        scratch_shapes=[
            pltpu.VMEM((heads, held_rows, width), jnp.bfloat16),
            pltpu.VMEM((groups, 2, (REACH + 1) * rows, width), jnp.bfloat16),
            pltpu.VMEM((groups, SPAN, width), jnp.bfloat16),
            pltpu.VMEM((groups, 2, SPAN, width), jnp.bfloat16),
            pltpu.VMEM((heads, held_rows, 2 * width), jnp.float32),
            pltpu.VMEM((heads, held_rows, width), jnp.bfloat16),
            pltpu.VMEM((2, heads, total_rows // width, width), jnp.float32),
            pltpu.VMEM((heads, 1, SPAN), jnp.float32),
            pltpu.VMEM((rows // BLOCK, SPAN, BLOCK), jnp.bfloat16),
            dma((groups, chips)),
            dma((groups, plane_size)),
            dma((groups, chips)),
            dma((REACH + 1, groups, plane_size)),
            dma((REACH, groups, plane_size)),
            dma((REACH + 1, groups, plane_size)),
            dma((groups,)),
            dma((groups,)),
            dma((groups, 2)),
            dma((groups, plane_size)),
            dma((groups, chips)),
        ],
        compiler_params=pltpu.CompilerParams(
            collective_id=0, has_side_effects=True, vmem_limit_bytes=36 * 1024 * 1024
        ),
        cost_estimate=pl.CostEstimate(
            flops=6 * pairs * width,
            transcendentals=2 * pairs,
            bytes_accessed=6 * chunk * head_count * width,
        ),
        name="attend",
    )(
        span_start.reshape(1, 1),
        steered_heads.reshape(1, -1),
        damping.reshape(-1, width),
        queries.transpose(1, 0, 2),
        key_value.transpose(2, 0, 1, 3),
    )
    return moved.transpose(1, 0, 2)


def solution(mesh):
    in_specs = (
        P(("prompt", "seq"), None, None),
        P(None, ("prompt", "seq"), None, None),
        P("prompt"),
        P("prompt"),
        P(),
    )
    out_specs = P(("prompt", "seq"), None, None)
    return jax.shard_map(
        per_device, mesh=mesh, in_specs=in_specs, out_specs=out_specs, check_vma=False
    )
```
